32 devices in a mesh: dp: 8 (over z, core), tensor: 4 (over y, x).
Axes of the slice: x: 2, y: 2, z: 4, core: 2. Of those that a mesh axis runs over, the one named last changes fastest.
Arguments:
- inputs: bfloat16 [8, 1024, 2048], P('dp'), may hold values from -6 to 6
- norm1_gain: float32 [2048], replicated, may hold values from 0.5 to 1.5
- norm1_shift: float32 [2048], replicated, may hold values from -3 to 3
- norm2_gain: float32 [2048], replicated, may hold values from 0.5 to 1.5
- norm2_shift: float32 [2048], replicated, may hold values from -3 to 3
- qkv_weight: bfloat16 [2048, 8, 3, 256], P(None, 'tensor'), may hold values from -0.125 to 0.125
- qkv_bias: float32 [8, 3, 256], P('tensor'), may hold values from -3 to 3
- dense_weight: bfloat16 [8, 256, 2048], P('tensor'), may hold values from -2 to 2
- fc_weight: bfloat16 [2048, 8192], P(None, 'tensor'), may hold values from -0.125 to 0.125
- fc_bias: float32 [8192], P('tensor'), may hold values from -3 to 3
- proj_weight: bfloat16 [8192, 2048], P('tensor'), may hold values from -0.0625 to 0.0625
- out_bias: float32 [2048], replicated, may hold values from -3 to 3
- picture_starts: int32 [8], P('dp'), may hold values from 0 to 768
- cotangent: bfloat16 [8, 1024, 2048], P('dp'), may hold values from -6 to 6
Outputs:
- output: bfloat16 [8, 1024, 2048], P('dp', 'tensor')
- input_grad: float32 [8, 1024, 2048], P('dp', 'tensor')
- norm1_gain_grad: float32 [2048], replicated
- norm1_shift_grad: float32 [2048], replicated
- norm2_gain_grad: float32 [2048], replicated
- norm2_shift_grad: float32 [2048], replicated
- qkv_weight_grad: float32 [2048, 8, 3, 256], P(None, 'tensor')
- qkv_bias_grad: float32 [8, 3, 256], P('tensor')
- dense_weight_grad: float32 [8, 256, 2048], P('tensor')
- fc_weight_grad: float32 [2048, 8192], P(None, 'tensor')
- fc_bias_grad: float32 [8192], P('tensor')
- proj_weight_grad: float32 [8192, 2048], P('tensor')
- out_bias_grad: float32 [2048], replicated
The draws below stay inside these ranges and needn't reach their ends.
Inputs may be any that keep to these rules, and one draw needn't show every extreme that they name: `picture_starts`: each sequence's picture span covers positions start to start + 255, inside the sequence.
All inputs are finite; a program needn't handle non-finite values.
Results may differ from the reference program's by a relative error of at most 0.012.
The reference program's roundings to bfloat16 on the way count: a program that leaves them out, or rounds other values in their place, can miss the bound.
Values sent between devices are 32-bit elements; how exact they have to be, the bound alone decides.
No kernel may reach another device: no remote copies, remote signals or barrier semaphores. Data moves between devices by JAX's collectives and lax.ppermute only.
A program may use at most 256 MiB of HBM per device.

```python
import jax
import jax.numpy as jnp
from jax import lax

D = 2048
HEADS = 8
HD = 256
ROT = 64
FF = 8192
LEN = 1024
PIC = 256
SEQS = 8


def place_ends(drawn, key, low, largest):
    place = [jax.random.randint(jax.random.fold_in(key, axis), (), 0, length) for axis, length in enumerate(drawn.shape)]
    main_axis = drawn.shape.index(max(drawn.shape))
    beside = place[:main_axis] + [(place[main_axis] + 1) % drawn.shape[main_axis]] + place[main_axis + 1:]
    return drawn.at[tuple(place)].set(low).at[tuple(beside)].set(largest)


def levels(own_key, extent, pieces, smallest, largest):
    factor_of, own = 1.0, jax.random.fold_in(own_key, 6)
    for dim, shards_of in pieces:
        draws = jnp.exp(jax.random.uniform(jax.random.fold_in(own, dim), (shards_of,), jnp.float32, smallest / len(pieces), largest / len(pieces)))
        factor_of = factor_of * jnp.repeat(draws, extent[dim] // shards_of).reshape([-1 if axis == dim else 1 for axis in range(len(extent))])
    return factor_of


def scatter_about(stream_key, extent, scale, most, split=(), held_as=jnp.bfloat16):
    factor_of = levels(stream_key, extent, split, -0.22, 0.18) if split else 1.0
    values = jax.random.normal(stream_key, extent, jnp.float32) * scale * factor_of
    return jnp.minimum(jnp.maximum(values, -most), most).astype(held_as)


def setup_inputs(seed: int = 0) -> dict:
    arg_keys = jax.random.split(jax.random.key(seed), 15)
    inputs = scatter_about(arg_keys[0], (SEQS, LEN, D), 1.0, 6.0, ((0, 8),))
    norm1_gain = jnp.clip(1.0 + 0.1 * jax.random.normal(arg_keys[1], (D,), jnp.float32), 0.5, 1.5)
    norm1_shift = scatter_about(arg_keys[2], (D,), 0.5, 3.0, (), jnp.float32)
    norm2_gain = jnp.clip(1.0 + 0.1 * jax.random.normal(arg_keys[3], (D,), jnp.float32), 0.5, 1.5)
    norm2_shift = scatter_about(arg_keys[4], (D,), 0.5, 3.0, (), jnp.float32)
    qkv_weight = scatter_about(arg_keys[5], (D, HEADS, 3, HD), D ** -0.5, 0.125, ((1, 4),))
    qkv_bias = scatter_about(arg_keys[6], (HEADS, 3, HD), 0.5, 3.0, ((0, 4),), jnp.float32)
    dense_weight = scatter_about(arg_keys[7], (HEADS, HD, D), (max(4 * D // LEN, 1)) ** -0.5, 2.0, ((0, 4),))
    fc_weight = scatter_about(arg_keys[8], (D, FF), D ** -0.5, 0.125, ((1, 4),))
    fc_bias = scatter_about(arg_keys[9], (FF,), 0.5, 3.0, ((0, 4),), jnp.float32)
    proj_weight = scatter_about(arg_keys[10], (FF, D), FF ** -0.5, 0.0625, ((0, 4),))
    out_bias = scatter_about(arg_keys[11], (D,), 0.5, 3.0, (), jnp.float32)
    picture_starts = place_ends(jax.random.randint(arg_keys[12], (SEQS,), 0, LEN - PIC + 1), jax.random.fold_in(arg_keys[12], 1), 0, LEN - PIC).astype(jnp.int32)
    cotangent = scatter_about(arg_keys[13], (SEQS, LEN, D), 1.0, 6.0, ((0, 8),))
    return {"inputs": inputs, "norm1_gain": norm1_gain, "norm1_shift": norm1_shift, "norm2_gain": norm2_gain, "norm2_shift": norm2_shift, "qkv_weight": qkv_weight, "qkv_bias": qkv_bias, "dense_weight": dense_weight, "fc_weight": fc_weight, "fc_bias": fc_bias, "proj_weight": proj_weight, "out_bias": out_bias, "picture_starts": picture_starts, "cotangent": cotangent}


NEG_LARGE = -1e+30
EPSILON = 1e-05

@jax.custom_vjp
def low(v):
    return lax.optimization_barrier(v.astype(jnp.bfloat16)).astype(jnp.float32)

@jax.custom_vjp
def low_back(v):
    return v

def low_keep(v):
    return (low(v), None)

def low_pass(kept, grad):
    return (grad,)

def back_keep(v):
    return (v, None)

def back_low(kept, grad):
    return (low(grad),)
low.defvjp(low_keep, low_pass)
low_back.defvjp(back_keep, back_low)

def precise_dot(left, right):
    return jnp.dot(left, right, precision=lax.Precision.HIGHEST)

def layer_norm(rows_in, norm_gain, norm_shift):
    average = lax.optimization_barrier(jnp.mean(rows_in, axis=-1, keepdims=True))
    centred = rows_in - average
    variance = lax.optimization_barrier(jnp.mean(centred * centred, axis=-1, keepdims=True))
    return centred * lax.rsqrt(variance + EPSILON) * norm_gain + norm_shift

def rotary_tables(length):
    half_dims = ROT // 2
    exponent = jnp.arange(half_dims, dtype=jnp.float32) * (2.0 / ROT)
    inverse = 1.0 / 10000.0 ** exponent
    angles = jnp.arange(length, dtype=jnp.float32)[:, None] * inverse[None, :]
    angles = jnp.concatenate([angles, angles], axis=1)
    return (jnp.cos(angles)[:, None, :], jnp.sin(angles)[:, None, :])

def rotate(operand, cosines, sines):
    turned = operand[..., :ROT]
    swapped = jnp.concatenate([-turned[..., ROT // 2:], turned[..., :ROT // 2]], axis=-1)
    return jnp.concatenate([turned * cosines + swapped * sines, operand[..., ROT:]], axis=-1)

def allowed_mask(row_pos, col_pos, span_start):
    causal = col_pos[None, :] <= row_pos[:, None]
    rows_inside = (row_pos >= span_start) & (row_pos < span_start + PIC)
    cols_inside = (col_pos >= span_start) & (col_pos < span_start + PIC)
    return causal | rows_inside[:, None] & cols_inside[None, :]

def block_sequence(rows_in, span_start, weights):
    gain_one, shift_one, gain_two, shift_two, qkv_w, qkv_b, dense_w, fc_w, fc_b, proj_w, bias_out = weights
    length = rows_in.shape[0]
    normed_attn = low(layer_norm(rows_in, gain_one, shift_one))
    normed_mlp = low(layer_norm(rows_in, gain_two, shift_two))
    projected = low_back(precise_dot(normed_attn, qkv_w.reshape(qkv_w.shape[0], -1)).reshape(length, HEADS, 3, HD) + qkv_b)
    cosines, sines = rotary_tables(length)
    queries = low(rotate(projected[:, :, 0], cosines, sines))
    key_rows = low(rotate(projected[:, :, 1], cosines, sines))
    value_rows = low(projected[:, :, 2])
    scores = low_back(jnp.einsum('qhd,khd->hqk', queries, key_rows, precision=lax.Precision.HIGHEST) * HD ** (-0.5))
    positions = jnp.arange(length)
    allowed = allowed_mask(positions, positions, span_start)
    weights_attn = low(jax.nn.softmax(jnp.where(allowed[None], scores, NEG_LARGE), axis=-1))
    context = low(low_back(jnp.einsum('hqk,khd->qhd', weights_attn, value_rows, precision=lax.Precision.HIGHEST)))
    attended = precise_dot(context.reshape(length, -1), dense_w.reshape(-1, dense_w.shape[-1]))
    hidden_pre = low_back(precise_dot(normed_mlp, fc_w) + fc_b)
    active = low(jax.nn.gelu(hidden_pre, approximate=False))
    return rows_in + attended + precise_dot(active, proj_w) + bias_out

def reference(inputs, norm1_gain, norm1_shift, norm2_gain, norm2_shift, qkv_weight, qkv_bias, dense_weight, fc_weight, fc_bias, proj_weight, out_bias, picture_starts, cotangent):
    params = (norm1_gain.astype(jnp.float32), norm1_shift.astype(jnp.float32), norm2_gain.astype(jnp.float32), norm2_shift.astype(jnp.float32), qkv_weight.astype(jnp.float32), qkv_bias.astype(jnp.float32), dense_weight.astype(jnp.float32), fc_weight.astype(jnp.float32), fc_bias.astype(jnp.float32), proj_weight.astype(jnp.float32), out_bias.astype(jnp.float32))

    def forward(inputs_f, weights):

        def one_sequence(running, seq_pair):
            return (running, jax.checkpoint(block_sequence)(seq_pair[0], seq_pair[1], weights))
        final_carry, results = lax.scan(one_sequence, jnp.zeros((), jnp.float32), (inputs_f, picture_starts))
        return results
    primal, pullback = jax.vjp(forward, inputs.astype(jnp.float32), params)
    input_grad, weight_grads = pullback(cotangent.astype(jnp.float32))
    gain_one_grad, shift_one_grad, gain_two_grad, shift_two_grad, qkv_w_grad, qkv_b_grad, dense_w_grad, fc_w_grad, fc_b_grad, proj_w_grad, bias_out_grad = weight_grads
    return (primal.astype(jnp.bfloat16), input_grad, gain_one_grad, shift_one_grad, gain_two_grad, shift_two_grad, qkv_w_grad, qkv_b_grad, dense_w_grad, fc_w_grad, fc_b_grad, proj_w_grad, bias_out_grad)
```

```python
import jax
import jax.numpy as jnp
from jax import lax
from jax.sharding import PartitionSpec as P

ROT = 64
PIC = 256

NEG_LARGE = -1e30
EPSILON = 1e-05


def rotary_tables(length):
    half_dims = ROT // 2
    exponent = jnp.arange(half_dims, dtype=jnp.float32) * (2.0 / ROT)
    inverse = 1.0 / 10000.0**exponent
    angles = jnp.arange(length, dtype=jnp.float32)[:, None] * inverse[None, :]
    return jnp.cos(angles), jnp.sin(angles)


def turn(rows, cosines, sines):
    half = ROT // 2
    first, second = rows[:, :half], rows[:, half:ROT]
    return jnp.concatenate(
        [first * cosines - second * sines, second * cosines + first * sines, rows[:, ROT:]], axis=1
    )


def allowed_mask(length, span_start):
    rows = lax.broadcasted_iota(jnp.int32, (length, length), 0)
    cols = lax.broadcasted_iota(jnp.int32, (length, length), 1)
    rows_inside = (rows >= span_start) & (rows < span_start + PIC)
    cols_inside = (cols >= span_start) & (cols < span_start + PIC)
    return (cols <= rows) | (rows_inside & cols_inside)


def norm_back(grad_rows, normed, inv_scale, norm_gain):
    grad_normed = grad_rows * norm_gain
    centre_term = jnp.mean(grad_normed, axis=-1, keepdims=True)
    slope_term = jnp.mean(grad_normed * normed, axis=-1, keepdims=True)
    return inv_scale * (grad_normed - centre_term - normed * slope_term)


def dot(left, right):
    return jnp.dot(left, right, preferred_element_type=jnp.float32)


def over_rows(left, right):
    return lax.dot_general(
        left, right, (((0,), (0,)), ((), ())), preferred_element_type=jnp.float32
    )


def against(left, right):
    return lax.dot_general(
        left, right, (((1,), (1,)), ((), ())), preferred_element_type=jnp.float32
    )


class LineSum:
    def __init__(self):
        ranks = lax.axis_size("dp")
        if ranks % 2 or (ranks > 2 and ranks % 4):
            raise ValueError("dp size")
        self.chips = ranks // 2
        index = lax.axis_index("dp")
        self.core = index % 2
        chip = index // 2
        self.side = [(rank, rank ^ 1) for rank in range(ranks)]
        self.stages = []
        last = self.chips - 1
        half = self.chips // 2
        for hop in range(half - 1):
            self.stages.append((self.both([(hop, hop + 1), (last - hop, last - hop - 1)]), None))
        if half:
            self.stages.append((self.both([(half - 1, half), (half, half - 1)]), None))
        for hop in reversed(range(half - 1)):
            receives = (chip == hop) | (chip == last - hop)
            self.stages.append(
                (self.both([(hop + 1, hop), (last - hop - 1, last - hop)]), receives)
            )

    def both(self, chip_pairs):
        return [(2 * a + core, 2 * b + core) for a, b in chip_pairs for core in range(2)]

    def send(self, value, stage):
        return lax.ppermute(value, "dp", self.stages[stage][0])

    def merge(self, value, received, stage):
        receives = self.stages[stage][1]
        return value + received if receives is None else jnp.where(receives, received, value)

    def swap(self, value):
        return lax.ppermute(value, "dp", self.side)


def tensor_sum(value):
    size = lax.axis_size("tensor")
    step = 1
    while step < size:
        value = value + lax.ppermute(value, "tensor", [(rank, rank ^ step) for rank in range(size)])
        step *= 2
    return value


def body(
    inputs,
    norm1_gain,
    norm1_shift,
    norm2_gain,
    norm2_shift,
    qkv_weight,
    qkv_bias,
    dense_weight,
    fc_weight,
    fc_bias,
    proj_weight,
    out_bias,
    picture_starts,
    cotangent,
):
    length, width = inputs.shape[1:]
    heads_here, head_dim = qkv_weight.shape[1], qkv_weight.shape[3]
    hidden = fc_weight.shape[1]
    span_start = picture_starts[0]
    score_scale = head_dim ** (-0.5)
    own_rows = length // lax.axis_size("tensor")
    row_start = lax.axis_index("tensor") * own_rows
    line = LineSum()
    depth = len(line.stages)
    env = {
        "x": inputs[0],
        "g": cotangent[0],
        "qkv_w": qkv_weight,
        "dense_w": dense_weight,
        "fc_w": fc_weight,
        "proj_w": proj_weight,
    }
    outs = {}
    ready = []
    done = {}

    def emit(name, row, value):
        ready.append((name, row, value))

    def normed_rows():
        return (env["x"].astype(jnp.float32) - env["mean"]) * env["inv"]

    rows_per_chunk = 256
    pieces = 4
    piece = hidden // pieces
    proj_rows = min(rows_per_chunk, piece)

    def work():
        rows_f = env["x"].astype(jnp.float32)
        env["mean"] = jnp.mean(rows_f, axis=-1, keepdims=True)
        centred = rows_f - env["mean"]
        env["inv"] = lax.rsqrt(jnp.mean(centred * centred, axis=-1, keepdims=True) + EPSILON)
        normed = normed_rows()
        env["mlp_in"] = (normed * norm2_gain + norm2_shift).astype(jnp.bfloat16)
        env["attn_in"] = (normed * norm1_gain + norm1_shift).astype(jnp.bfloat16)
        outs["proj"] = jnp.zeros((hidden, width), jnp.float32)
        for p in range(pieces):
            part = slice(p * piece, (p + 1) * piece)
            pre = dot(env["mlp_in"], env["fc_w"][:, part]) + fc_bias[part]
            env["active", p] = jax.nn.gelu(pre, approximate=False).astype(jnp.bfloat16)
            env["pre", p] = pre
            for r in range(0, piece, proj_rows):
                emit(
                    "proj",
                    p * piece + r,
                    over_rows(env["active", p][:, r : r + proj_rows], env["g"]),
                )
                yield 3 if p or r else 0
            yield 9
            if p == 0:
                continue
            for b in [0, 1] if p == 1 else [p]:
                part = slice(b * piece, (b + 1) * piece)
                active_grad = against(env["g"], env["proj_w"][part])
                unused, gelu_back = jax.vjp(
                    lambda operand: jax.nn.gelu(operand, approximate=False), env.pop(("pre", b))
                )
                env["pre_grad", b] = gelu_back(active_grad)[0].astype(jnp.bfloat16)
                yield 9
        env["pre_grad"] = jnp.concatenate(
            [env.pop(("pre_grad", p)) for p in range(pieces)], axis=1
        )
        env["active"] = jnp.concatenate([env.pop(("active", p)) for p in range(pieces)], axis=1)
        outs["fc"] = jnp.zeros((width, hidden), jnp.float32)
        fc_rows = min(rows_per_chunk, width)

        def fc_chunk(r):
            emit("fc", r, over_rows(env["mlp_in"][:, r : r + fc_rows], env["pre_grad"]))

        def attention():
            qkv_flat = env.pop("qkv_w").reshape(width, heads_here * 3 * head_dim)
            env["qkv_flat"] = qkv_flat
            yield 10
            projected = dot(env["attn_in"], env["qkv_flat"]) + qkv_bias.reshape(1, -1)
            cosines, sines = rotary_tables(length)
            for h in range(heads_here):
                base = h * 3 * head_dim
                env["q", h] = turn(projected[:, base : base + head_dim], cosines, sines).astype(
                    jnp.bfloat16
                )
                env["k", h] = turn(
                    projected[:, base + head_dim : base + 2 * head_dim], cosines, sines
                ).astype(jnp.bfloat16)
                env["v", h] = projected[:, base + 2 * head_dim : base + 3 * head_dim].astype(
                    jnp.bfloat16
                )
            yield 14
            for h in range(heads_here):
                scores = against(env["q", h], env["k", h]) * score_scale
                scores = jnp.where(allowed_mask(length, span_start), scores, NEG_LARGE)
                exponent = jnp.exp(scores - jnp.max(scores, axis=-1, keepdims=True))
                probabilities = exponent / jnp.sum(exponent, axis=-1, keepdims=True)
                env["p", h] = probabilities
                env["context", h] = dot(probabilities.astype(jnp.bfloat16), env["v", h]).astype(
                    jnp.bfloat16
                )
                yield 10
            env["context"] = jnp.concatenate(
                [env.pop(("context", h)) for h in range(heads_here)], axis=1
            )
            env["dense_flat"] = env.pop("dense_w").reshape(heads_here * head_dim, width)
            env["attended"] = dot(env["context"], env["dense_flat"])
            context_grad = against(env["g"], env["dense_flat"]).astype(jnp.bfloat16)
            for h in range(heads_here):
                env["cg", h] = context_grad[:, h * head_dim : (h + 1) * head_dim]
            yield 8
            summed = lax.psum_scatter(
                env.pop("attended") + dot(env.pop("active"), env["proj_w"]),
                "tensor",
                scatter_dimension=0,
                tiled=True,
            )
            own_inputs = lax.dynamic_slice_in_dim(env["x"], row_start, own_rows, 0)
            done["output"] = (own_inputs.astype(jnp.float32) + summed + out_bias).astype(
                jnp.bfloat16
            )[None]
            yield 14
            for h in range(heads_here):
                grad = env.pop(("cg", h))
                probabilities = env.pop(("p", h))
                prob_grad = against(grad, env.pop(("v", h)))
                row_dot = jnp.sum(prob_grad * probabilities, axis=-1, keepdims=True)
                score_grad = (probabilities * (prob_grad - row_dot)).astype(jnp.bfloat16)
                query_grad = dot(score_grad, env.pop(("k", h))) * score_scale
                key_grad = over_rows(score_grad, env.pop(("q", h))) * score_scale
                value_grad = over_rows(probabilities.astype(jnp.bfloat16), grad)
                cosines, sines = rotary_tables(length)
                env["flat", h] = jnp.concatenate(
                    [
                        turn(query_grad, cosines, -sines),
                        turn(key_grad, cosines, -sines),
                        value_grad,
                    ],
                    axis=1,
                ).astype(jnp.bfloat16)
                yield 15
            env["flat"] = jnp.concatenate([env.pop(("flat", h)) for h in range(heads_here)], axis=1)

        inner = attention()
        for r in range(0, width, fc_rows):
            fc_chunk(r)
            yield 3
            for cost in inner:
                yield cost
                if len(ready) == 0:
                    break
        for cost in inner:
            yield cost
        outs["dense"] = jnp.zeros((heads_here * head_dim, width), jnp.float32)
        dense_rows = min(rows_per_chunk, heads_here * head_dim)
        for r in range(0, heads_here * head_dim, dense_rows):
            emit("dense", r, over_rows(env["context"][:, r : r + dense_rows], env["g"]))
            yield 3
        outs["qkv"] = jnp.zeros((width, heads_here, 3, head_dim), jnp.float32)

        def qkv_chunk(r):
            emit("qkv", r, over_rows(env["attn_in"][:, r : r + fc_rows], env["flat"]))

        def finish():
            mlp_in_grad = against(env["pre_grad"], env["fc_w"])
            env["mlp_in_grad"] = mlp_in_grad
            yield 12
            attn_in_grad = against(env["flat"], env["qkv_flat"])
            env["attn_in_grad"] = attn_in_grad
            yield 10
            normed = normed_rows()
            mlp_in_grad, attn_in_grad = env["mlp_in_grad"], env["attn_in_grad"]
            input_part = norm_back(attn_in_grad, normed, env["inv"], norm1_gain) + norm_back(
                mlp_in_grad, normed, env["inv"], norm2_gain
            )
            own_grad = lax.psum_scatter(input_part, "tensor", scatter_dimension=0, tiled=True)
            own_cot = lax.dynamic_slice_in_dim(env["g"], row_start, own_rows, 0)
            done["input_grad"] = (own_grad + own_cot.astype(jnp.float32))[None]
            yield 10
            normed = normed_rows()
            mlp_in_grad, attn_in_grad = env.pop("mlp_in_grad"), env.pop("attn_in_grad")
            env["norm_sums"] = jnp.stack(
                [
                    jnp.sum(attn_in_grad * normed, axis=0),
                    jnp.sum(attn_in_grad, axis=0),
                    jnp.sum(mlp_in_grad * normed, axis=0),
                    jnp.sum(mlp_in_grad, axis=0),
                ]
            )
            yield 10
            env["norm_sums"] = tensor_sum(env["norm_sums"])
            yield 8
            biases = jnp.concatenate(
                [
                    jnp.sum(env["g"].astype(jnp.float32), axis=0),
                    jnp.sum(env["pre_grad"].astype(jnp.float32), axis=0),
                    jnp.sum(env["flat"].astype(jnp.float32), axis=0),
                ]
            )
            flat = jnp.concatenate([env.pop("norm_sums").reshape(-1), biases])
            lanes = 1024
            rows = -(-flat.shape[0] // (lanes * 16)) * 16
            flat = jnp.pad(flat, (0, rows * lanes - flat.shape[0])).reshape(rows, lanes)
            outs["small"] = jnp.zeros((rows, lanes), jnp.float32)
            emit("small", 0, flat)
            yield 8

        inner = finish()
        for r in range(0, width, fc_rows):
            qkv_chunk(r)
            yield 3
            for cost in inner:
                yield cost
                if len(ready) == 0:
                    break
        for cost in inner:
            yield cost

    steps = work()
    exhausted = [False]

    def advance():
        try:
            return next(steps)
        except StopIteration:
            exhausted[0] = True
            return 0

    def split(value):
        rows = value.shape[0] // 2
        own = lax.dynamic_slice_in_dim(value, line.core * rows, rows, 0)
        other = lax.dynamic_slice_in_dim(value, (1 - line.core) * rows, rows, 0)
        return own + line.swap(other)

    def place(name, row, rows, own, other):
        target = outs[name]
        core = line.core
        for value, which in ((own, core), (other, 1 - core)):
            block = value.reshape((rows,) + target.shape[1:])
            target = lax.dynamic_update_slice_in_dim(target, block, row + which * rows, 0)
        outs[name] = target

    live = []
    slot_budget = 14.0
    while not ready:
        advance()
    while True:
        if ready:
            name, row, value = ready.pop(0)
            live.append(
                {
                    "name": name,
                    "row": row,
                    "rows": value.shape[0] // 2,
                    "age": 0,
                    "value": split(value),
                }
            )
        spent = 0.0
        while not exhausted[0] and (spent < slot_budget or not ready):
            spent += advance()
        keep = []
        for chunk in live:
            age = chunk["age"]
            chunk["age"] += 1
            if age == 0:
                keep.append(chunk)
                continue
            stage = age - 1
            if 0 < stage <= depth:
                chunk["value"] = line.merge(chunk["value"], chunk.pop("wait"), stage - 1)
            if stage < depth:
                chunk["wait"] = line.send(chunk["value"], stage)
            elif stage == depth:
                chunk["wait"] = line.swap(chunk["value"])
            else:
                place(
                    chunk["name"], chunk["row"], chunk["rows"], chunk["value"], chunk.pop("wait")
                )
                continue
            keep.append(chunk)
        live = keep
        if not live and not ready and exhausted[0]:
            break
        names = list(env)
        tied = lax.optimization_barrier(
            ([env[n] for n in names], outs, [c["value"] for c in live], ready_values(ready))
        )
        env_new, outs_new, values, ready_new = tied
        env.update(zip(names, env_new))
        outs.update(outs_new)
        for chunk, value in zip(live, values):
            chunk["value"] = value
        ready[:] = [(n, r, v) for (n, r, unused), v in zip(ready, ready_new)]

    small = outs["small"].reshape(-1)
    sizes = [width] * 4 + [width, hidden, heads_here * 3 * head_dim]
    parts = []
    start = 0
    for size in sizes:
        parts.append(small[start : start + size])
        start += size
    return (
        done["output"],
        done["input_grad"],
        parts[0],
        parts[1],
        parts[2],
        parts[3],
        outs["qkv"],
        parts[6].reshape(heads_here, 3, head_dim),
        outs["dense"].reshape(heads_here, head_dim, width),
        outs["fc"],
        parts[5],
        outs["proj"],
        parts[4],
    )


def ready_values(ready):
    return [value for unused_name, unused_row, value in ready]


def solution(mesh):
    return jax.shard_map(
        body,
        mesh=mesh,
        in_specs=(
            P("dp", None, None),
            P(),
            P(),
            P(),
            P(),
            P(None, "tensor", None, None),
            P("tensor", None, None),
            P("tensor", None, None),
            P(None, "tensor"),
            P("tensor"),
            P("tensor", None),
            P(),
            P("dp"),
            P("dp", None, None),
        ),
        out_specs=(
            P("dp", "tensor", None),
            P("dp", "tensor", None),
            P(),
            P(),
            P(),
            P(),
            P(None, "tensor", None, None),
            P("tensor", None, None),
            P("tensor", None, None),
            P(None, "tensor"),
            P("tensor"),
            P("tensor", None),
            P(),
        ),
        check_vma=False,
    )
```

```python
import jax
import jax.numpy as jnp
import numpy as np
from jax import lax
from jax.experimental import pallas as pl
from jax.experimental.pallas import tpu as pltpu
from jax.sharding import PartitionSpec as P

ROT = 64
PIC = 256

NEG_LARGE = -1e30
EPSILON = 1e-05
SLOT_BUDGET = 12.0


def rotary_tables(length):
    half_dims = ROT // 2
    exponent = jnp.arange(half_dims, dtype=jnp.float32) * (2.0 / ROT)
    inverse = 1.0 / 10000.0**exponent
    angles = jnp.arange(length, dtype=jnp.float32)[:, None] * inverse[None, :]
    return jnp.cos(angles), jnp.sin(angles)


def turn(rows, cosines, sines):
    half = ROT // 2
    first, second = rows[:, :half], rows[:, half:ROT]
    return jnp.concatenate(
        [first * cosines - second * sines, second * cosines + first * sines, rows[:, ROT:]], axis=1
    )


def allowed_mask(length, span_start):
    rows = lax.broadcasted_iota(jnp.int32, (length, length), 0)
    cols = lax.broadcasted_iota(jnp.int32, (length, length), 1)
    rows_inside = (rows >= span_start) & (rows < span_start + PIC)
    cols_inside = (cols >= span_start) & (cols < span_start + PIC)
    return (cols <= rows) | (rows_inside & cols_inside)


def norm_back(grad_rows, normed, inv_scale, norm_gain):
    grad_normed = grad_rows * norm_gain
    centre_term = jnp.mean(grad_normed, axis=-1, keepdims=True)
    slope_term = jnp.mean(grad_normed * normed, axis=-1, keepdims=True)
    return inv_scale * (grad_normed - centre_term - normed * slope_term)


def dot(left, right):
    return jnp.dot(left, right, preferred_element_type=jnp.float32)


def over_rows(left, right):
    return lax.dot_general(
        left, right, (((0,), (0,)), ((), ())), preferred_element_type=jnp.float32
    )


def against(left, right):
    return lax.dot_general(
        left, right, (((1,), (1,)), ((), ())), preferred_element_type=jnp.float32
    )


class LineSum:
    def __init__(self):
        ranks = lax.axis_size("dp")
        if ranks % 2 or (ranks > 2 and ranks % 4):
            raise ValueError("dp size")
        self.chips = ranks // 2
        index = lax.axis_index("dp")
        self.core = index % 2
        chip = index // 2
        self.side = [(rank, rank ^ 1) for rank in range(ranks)]
        self.stages = []
        last = self.chips - 1
        half = self.chips // 2
        for hop in range(half - 1):
            self.stages.append((self.both([(hop, hop + 1), (last - hop, last - hop - 1)]), None))
        if half:
            self.stages.append((self.both([(half - 1, half), (half, half - 1)]), None))
        for hop in reversed(range(half - 1)):
            receives = (chip == hop) | (chip == last - hop)
            self.stages.append(
                (self.both([(hop + 1, hop), (last - hop - 1, last - hop)]), receives)
            )

    def both(self, chip_pairs):
        return [(2 * a + core, 2 * b + core) for a, b in chip_pairs for core in range(2)]

    def send(self, value, stage):
        return lax.ppermute(value, "dp", self.stages[stage][0])

    def merge(self, value, received, stage):
        receives = self.stages[stage][1]
        return value + received if receives is None else jnp.where(receives, received, value)

    def swap(self, value):
        return lax.ppermute(value, "dp", self.side)


def empty(name, shape):
    return pl.pallas_call(
        lambda out_ref: None,
        out_shape=jax.ShapeDtypeStruct(shape, jnp.float32),
        out_specs=pl.BlockSpec(memory_space=pl.ANY),
        name=name,
    )()


def copy_in(target, own, other, core, offset, half):
    rows = own.shape[0]

    def kernel(core_ref, own_ref, other_ref, unused_ref, out_ref, sems):
        mine = core_ref[0]
        copies = [
            pltpu.make_async_copy(
                source,
                out_ref.at[pl.ds(pl.multiple_of(offset + which * half, 8), rows)],
                sems.at[index],
            )
            for index, (source, which) in enumerate(((own_ref, mine), (other_ref, 1 - mine)))
        ]
        for copy in copies:
            copy.start()
        for copy in copies:
            copy.wait()

    anywhere = pl.BlockSpec(memory_space=pl.ANY)
    return pl.pallas_call(
        kernel,
        out_shape=jax.ShapeDtypeStruct(target.shape, target.dtype),
        grid_spec=pltpu.PrefetchScalarGridSpec(
            num_scalar_prefetch=1,
            grid=(),
            in_specs=[anywhere, anywhere, anywhere],
            out_specs=anywhere,
            scratch_shapes=[pltpu.SemaphoreType.DMA((2,))],
        ),
        input_output_aliases={3: 0},
        name="copy_in",
    )(core.reshape(1).astype(jnp.int32), own, other, target)


def tensor_sum(value):
    size = lax.axis_size("tensor")
    step = 1
    while step < size:
        value = value + lax.ppermute(value, "tensor", [(rank, rank ^ step) for rank in range(size)])
        step *= 2
    return value


def body(
    inputs,
    norm1_gain,
    norm1_shift,
    norm2_gain,
    norm2_shift,
    qkv_weight,
    qkv_bias,
    dense_weight,
    fc_weight,
    fc_bias,
    proj_weight,
    out_bias,
    picture_starts,
    cotangent,
):
    length, width = inputs.shape[1:]
    heads_here, head_dim = qkv_weight.shape[1], qkv_weight.shape[3]
    hidden = fc_weight.shape[1]
    span_start = picture_starts[0]
    score_scale = head_dim ** (-0.5)
    own_rows = length // lax.axis_size("tensor")
    row_start = lax.axis_index("tensor") * own_rows
    line = LineSum()
    depth = len(line.stages)
    env = {
        "x": inputs[0],
        "g": cotangent[0],
        "qkv_w": qkv_weight,
        "dense_w": dense_weight,
        "fc_w": fc_weight,
        "proj_w": proj_weight,
    }
    outs = {}
    ready = []
    done = {}
    first_core = line.core == 0

    def halves(key, low, high):
        env[key + "_own"] = jnp.where(first_core, low, high)
        env[key + "_other"] = jnp.where(first_core, high, low)

    def emit(name, offset, left, right, start, rows, drop=()):
        ready.append(
            {
                "name": name,
                "offset": offset,
                "left": left,
                "right": right,
                "start": start,
                "rows": rows,
                "drop": drop,
            }
        )

    def normed_rows():
        return (env["x"].astype(jnp.float32) - env["mean"]) * env["inv"]

    rows_per_chunk = 128
    half_hidden = hidden // 2

    def work():
        rows_f = env["x"].astype(jnp.float32)
        env["mean"] = jnp.mean(rows_f, axis=-1, keepdims=True)
        centred = rows_f - env["mean"]
        env["inv"] = lax.rsqrt(jnp.mean(centred * centred, axis=-1, keepdims=True) + EPSILON)
        normed = normed_rows()
        env["mlp_in"] = (normed * norm2_gain + norm2_shift).astype(jnp.bfloat16)
        env["attn_in"] = (normed * norm1_gain + norm1_shift).astype(jnp.bfloat16)
        outs["proj"] = empty("proj_buffer", (hidden, width))
        cuts = [0, half_hidden // 8] + [half_hidden * q // 4 for q in range(1, 5)]
        groups = len(cuts) - 1

        def pick(array, axis, q):
            low = lax.slice_in_dim(array, cuts[q], cuts[q + 1], axis=axis)
            high = lax.slice_in_dim(
                array, half_hidden + cuts[q], half_hidden + cuts[q + 1], axis=axis
            )
            return jnp.concatenate([low, high], axis=axis)

        def backward(q):
            active_grad = against(env["g"], pick(env["proj_w"], 0, q))
            env[f"pre_grad{q}"] = (active_grad * env.pop(f"slope{q}")).astype(jnp.bfloat16)

        for q in range(groups):
            size = cuts[q + 1] - cuts[q]
            pre = dot(env["mlp_in"], pick(env["fc_w"], 1, q)) + pick(fc_bias, 0, q)
            below = 0.5 * lax.erfc(pre * -np.float32(np.sqrt(0.5)))
            active = (pre * below).astype(jnp.bfloat16)
            density = jnp.exp(-0.5 * pre * pre) * np.float32(1.0 / np.sqrt(2.0 * np.pi))
            env[f"slope{q}"] = below + pre * density
            env[f"active{q}"] = active
            halves(f"active{q}", active[:, :size], active[:, size:])
            step = min(rows_per_chunk, size)
            for r in range(0, size, step):
                emit("proj", cuts[q] + r, f"active{q}", "g", r, step)
            yield 9 * size * 4 / half_hidden
            if q >= 2:
                for b in range(3) if q == 2 else [q]:
                    backward(b)
                    yield 7 * (cuts[b + 1] - cuts[b]) * 4 / half_hidden

        def whole(prefix):
            parts = [env.pop(f"{prefix}{q}") for q in range(groups)]
            lows = [part[:, : part.shape[1] // 2] for part in parts]
            highs = [part[:, part.shape[1] // 2 :] for part in parts]
            return jnp.concatenate(lows + highs, axis=1)

        env["pre_grad"] = whole("pre_grad")
        env["active"] = whole("active")
        outs["fc"] = empty("fc_buffer", (width, hidden))
        half_width = width // 2
        halves("mlp", env["mlp_in"][:, :half_width], env["mlp_in"][:, half_width:])
        step = min(rows_per_chunk, half_width)
        for r in range(0, half_width, step):
            emit("fc", r, "mlp", "pre_grad", r, step)
        yield 8

        qkv_flat = env.pop("qkv_w").reshape(width, heads_here * 3 * head_dim)
        env["qkv_flat"] = qkv_flat
        yield 12
        projected = dot(env["attn_in"], env["qkv_flat"]) + qkv_bias.reshape(1, -1)
        cosines, sines = rotary_tables(length)
        for h in range(heads_here):
            base = h * 3 * head_dim
            env[f"q{h}"] = turn(projected[:, base : base + head_dim], cosines, sines).astype(
                jnp.bfloat16
            )
            env[f"k{h}"] = turn(
                projected[:, base + head_dim : base + 2 * head_dim], cosines, sines
            ).astype(jnp.bfloat16)
            env[f"v{h}"] = projected[:, base + 2 * head_dim : base + 3 * head_dim].astype(
                jnp.bfloat16
            )
        yield 14
        for h in range(heads_here):
            scores = against(env[f"q{h}"], env[f"k{h}"]) * score_scale
            scores = jnp.where(allowed_mask(length, span_start), scores, NEG_LARGE)
            exponent = jnp.exp(scores - jnp.max(scores, axis=-1, keepdims=True))
            probabilities = exponent / jnp.sum(exponent, axis=-1, keepdims=True)
            env[f"p{h}"] = probabilities
            env[f"context{h}"] = dot(probabilities.astype(jnp.bfloat16), env[f"v{h}"]).astype(
                jnp.bfloat16
            )
            yield 10
        context = jnp.concatenate([env.pop(f"context{h}") for h in range(heads_here)], axis=1)
        inner = heads_here * head_dim
        env["dense_flat"] = env.pop("dense_w").reshape(inner, width)
        env["attended"] = dot(context, env["dense_flat"])
        halves("context", context[:, : inner // 2], context[:, inner // 2 :])
        context_grad = against(env["g"], env["dense_flat"]).astype(jnp.bfloat16)
        for h in range(heads_here):
            env[f"cg{h}"] = context_grad[:, h * head_dim : (h + 1) * head_dim]
        outs["dense"] = empty("dense_buffer", (inner, width))
        step = min(rows_per_chunk, inner // 2)
        for r in range(0, inner // 2, step):
            emit("dense", r, "context", "g", r, step)
        yield 10
        summed = lax.psum_scatter(
            env.pop("attended") + dot(env.pop("active"), env["proj_w"]),
            "tensor",
            scatter_dimension=0,
            tiled=True,
        )
        yield 14
        for h in range(heads_here):
            grad = env.pop(f"cg{h}")
            probabilities = env.pop(f"p{h}")
            prob_grad = against(grad, env.pop(f"v{h}"))
            row_dot = jnp.sum(prob_grad * probabilities, axis=-1, keepdims=True)
            score_grad = (probabilities * (prob_grad - row_dot)).astype(jnp.bfloat16)
            query_grad = dot(score_grad, env.pop(f"k{h}")) * score_scale
            key_grad = over_rows(score_grad, env.pop(f"q{h}")) * score_scale
            value_grad = over_rows(probabilities.astype(jnp.bfloat16), grad)
            cosines, sines = rotary_tables(length)
            env[f"flat{h}"] = jnp.concatenate(
                [
                    turn(query_grad, cosines, -sines),
                    turn(key_grad, cosines, -sines),
                    value_grad,
                ],
                axis=1,
            ).astype(jnp.bfloat16)
            yield 15
        env["flat"] = jnp.concatenate([env.pop(f"flat{h}") for h in range(heads_here)], axis=1)
        halves("attn", env["attn_in"][:, :half_width], env["attn_in"][:, half_width:])
        outs["qkv"] = jnp.zeros((width, heads_here, 3, head_dim), jnp.float32)
        step = min(rows_per_chunk, half_width)
        sizes = [step] * (half_width // step)
        if step % 64 == 0:
            sizes = sizes[:-1] + [step // 2, step // 4, step // 4]
        r = 0
        for size in sizes:
            emit("qkv", r, "attn", "flat", r, size)
            r += size
        yield 8
        env["mlp_in_grad"] = against(env["pre_grad"], env["fc_w"])
        yield 12
        env["attn_in_grad"] = against(env["flat"], env["qkv_flat"])
        yield 10
        normed = normed_rows()
        mlp_in_grad, attn_in_grad = env["mlp_in_grad"], env["attn_in_grad"]
        input_part = norm_back(attn_in_grad, normed, env["inv"], norm1_gain) + norm_back(
            mlp_in_grad, normed, env["inv"], norm2_gain
        )
        own_inputs = lax.dynamic_slice_in_dim(env["x"], row_start, own_rows, 0)
        done["output"] = (own_inputs.astype(jnp.float32) + summed + out_bias).astype(
            jnp.bfloat16
        )[None]
        own_grad = lax.psum_scatter(input_part, "tensor", scatter_dimension=0, tiled=True)
        env["norm_sums"] = jnp.stack(
            [
                jnp.sum(attn_in_grad * normed, axis=0),
                jnp.sum(attn_in_grad, axis=0),
                jnp.sum(mlp_in_grad * normed, axis=0),
                jnp.sum(mlp_in_grad, axis=0),
            ]
        )
        env.pop("mlp_in_grad")
        env.pop("attn_in_grad")
        yield 25
        env["norm_sums"] = tensor_sum(env["norm_sums"])
        yield 8
        biases = jnp.concatenate(
            [
                jnp.sum(env["g"].astype(jnp.float32), axis=0),
                jnp.sum(env["pre_grad"].astype(jnp.float32), axis=0),
                jnp.sum(env["flat"].astype(jnp.float32), axis=0),
            ]
        )
        flat = jnp.concatenate([env.pop("norm_sums").reshape(-1), biases])
        lanes = 1024
        rows = -(-flat.shape[0] // (lanes * 16)) * 16
        env["small"] = jnp.pad(flat, (0, rows * lanes - flat.shape[0])).reshape(rows, lanes)
        outs["small"] = jnp.zeros((rows, lanes), jnp.float32)
        emit("small", 0, "small", None, 0, rows // 2)
        ready.insert(0, ready.pop())
        for unused in range(4):
            yield 14
        own_cot = lax.dynamic_slice_in_dim(env["g"], row_start, own_rows, 0)
        done["input_grad"] = (own_grad + own_cot.astype(jnp.float32))[None]

    steps = work()
    exhausted = [False]

    def advance():
        try:
            return next(steps)
        except StopIteration:
            exhausted[0] = True
            return 0

    def first_sum(item):
        if item["right"] is None:
            value, rows = env[item["left"]], item["rows"]
            own = lax.dynamic_slice_in_dim(value, line.core * rows, rows, 0)
            other = lax.dynamic_slice_in_dim(value, (1 - line.core) * rows, rows, 0)
            return own + line.swap(other)
        part = slice(item["start"], item["start"] + item["rows"])
        right = env[item["right"]]
        received = line.swap(over_rows(env[item["left"] + "_other"][:, part], right))
        return over_rows(env[item["left"] + "_own"][:, part], right) + received

    def place(item, own, other):
        name, rows = item["name"], item["rows"]
        target = outs[name]
        half = target.shape[0] // 2
        if target.ndim == 2 and name != "small":
            outs[name] = copy_in(target, own, other, line.core, item["offset"], half)
            return
        for value, which in ((own, line.core), (other, 1 - line.core)):
            block = value.reshape((rows,) + target.shape[1:])
            target = lax.dynamic_update_slice_in_dim(
                target, block, item["offset"] + which * half, 0
            )
        outs[name] = target

    live = []
    slot = 0
    while not ready:
        advance()
    while True:
        if ready:
            item = ready.pop(0)
            item["age"] = 0
            item["value"] = first_sum(item)
            live.append(item)
        spent = 0.0
        while not exhausted[0] and (spent < SLOT_BUDGET or not ready):
            if slot == 0 and ready:
                break
            spent += advance()
        slot += 1
        keep = []
        for item in live:
            age = item["age"]
            item["age"] += 1
            if age == 0:
                keep.append(item)
                continue
            stage = age - 1
            if 0 < stage <= depth:
                item["value"] = line.merge(item["value"], item.pop("wait"), stage - 1)
            if stage < depth:
                item["wait"] = line.send(item["value"], stage)
            elif stage == depth:
                item["wait"] = line.swap(item["value"])
            else:
                place(item, item["value"], item.pop("wait"))
                continue
            keep.append(item)
        live = keep
        if not live and not ready and exhausted[0]:
            break
        names = list(env)
        tied = lax.optimization_barrier(
            ([env[n] for n in names], outs, done, [item["value"] for item in live])
        )
        env.update(zip(names, tied[0]))
        outs.update(tied[1])
        done.update(tied[2])
        for item, value in zip(live, tied[3]):
            item["value"] = value

    small = outs["small"].reshape(-1)
    sizes = [width] * 4 + [width, hidden, heads_here * 3 * head_dim]
    parts = []
    start = 0
    for size in sizes:
        parts.append(small[start : start + size])
        start += size
    return (
        done["output"],
        done["input_grad"],
        parts[0],
        parts[1],
        parts[2],
        parts[3],
        outs["qkv"],
        parts[6].reshape(heads_here, 3, head_dim),
        outs["dense"].reshape(heads_here, head_dim, width),
        outs["fc"],
        parts[5],
        outs["proj"],
        parts[4],
    )


def solution(mesh):
    return jax.shard_map(
        body,
        mesh=mesh,
        in_specs=(
            P("dp", None, None),
            P(),
            P(),
            P(),
            P(),
            P(None, "tensor", None, None),
            P("tensor", None, None),
            P("tensor", None, None),
            P(None, "tensor"),
            P("tensor"),
            P("tensor", None),
            P(),
            P("dp"),
            P("dp", None, None),
        ),
        out_specs=(
            P("dp", "tensor", None),
            P("dp", "tensor", None),
            P(),
            P(),
            P(),
            P(),
            P(None, "tensor", None, None),
            P("tensor", None, None),
            P("tensor", None, None),
            P(None, "tensor"),
            P("tensor"),
            P("tensor", None),
            P(),
        ),
        check_vma=False,
    )
```
